32 devices in a mesh: px: 8 (over z, y), py: 4 (over x, core).
Axes of the slice: x: 2, y: 2, z: 4, core: 2. Of those that a mesh axis runs over, the one named last changes fastest.
Arguments:
- history: bfloat16 [8, 4, 3, 128, 384], P('px', 'py'), may hold values from -6 to 6
- incident: float32 [8, 4, 4, 128, 384], P('px', 'py'), may hold values from -6 to 6
- blocks: bfloat16 [8, 4, 32, 128, 128], P('px', 'py'), may hold values from -0.09375 to 0.09375
- self_inverse: float32 [8, 4, 128, 128], P('px', 'py'), as said below
- neighbour: int32 [8, 4, 32], P('px', 'py'), may hold values from 0 to 8
- delay: int32 [8, 4, 32], P('px', 'py'), may hold values from 1 to 3
Outputs:
- currents: bfloat16 [8, 4, 4, 128, 384], P('px', 'py')
The draws below stay inside these ranges and needn't reach their ends.
Inputs may be any that keep to these rules, and one draw needn't show every extreme that they name: neighbour n names the source tile at row offset n // 3 - 1 and column offset n % 3 - 1. `self_inverse`: each matrix has a positive diagonal.
All inputs are finite; a program needn't handle non-finite values.
Results may differ from the reference program's by a relative error of at most 0.004.
Values may be sent and summed in bfloat16 or wider, within the bound.
A program may use at most 64 MiB of HBM per device.

```python
import jax
import jax.numpy as jnp
from jax import lax

B = 128
P_SIZE = 384
NBLK = 32
DMAX = 3
STEPS = 4
NTX = 8
NTY = 4


def draw_self_inverse(key, part):
    first, second = jax.random.split(jax.random.fold_in(key, 17))
    shape = (NTX, NTY, B, B)
    diag = jax.random.uniform(first, (NTX, NTY, B), jnp.float32, 0.6, 1.4)
    off = jax.random.normal(second, shape, jnp.float32) * (0.5 / B ** 0.5)
    eye = jnp.eye(B, dtype=jnp.float32)
    return off * (1.0 - eye) + diag[..., None] * eye


def plant(array, stream_key, least, high):
    longest = array.shape.index(max(array.shape))
    spots = []
    for shift in (0, 1):
        where = [jax.random.randint(jax.random.fold_in(stream_key, axis), (), 0, length) for axis, length in enumerate(array.shape)]
        where[longest] = (where[longest] + shift) % array.shape[longest]
        spots.append(tuple(where))
    return array.at[spots[0]].set(least).at[spots[1]].set(high)


def level_of(key, dims, cuts, least, largest):
    def one(position, parts):
        heights = jax.random.uniform(jax.random.fold_in(jax.random.fold_in(key, 6), position), (parts,), jnp.float32, least / len(cuts), largest / len(cuts))
        return jnp.repeat(jnp.exp(heights), dims[position] // parts).reshape((-1,) + (1,) * (len(dims) - position - 1))

    level = one(*cuts[0])
    for cut in cuts[1:]:
        level = level * one(*cut)
    return level


def gaussian(stream_key, extent, deviation, reach, cuts=(), kind=jnp.bfloat16):
    values = deviation * jax.random.normal(stream_key, extent, jnp.float32)
    if cuts:
        values = values * level_of(stream_key, extent, cuts, -0.22, 0.18)
    return jnp.clip(values, -reach, reach).astype(kind)


def setup_inputs(seed: int = 0) -> dict:
    splits = jax.random.split(jax.random.key(seed), 7)
    return {
        "history": gaussian(splits[0], (NTX, NTY, DMAX, B, P_SIZE), 1.0, 6.0, ((0, 8), (1, 4))),
        "incident": gaussian(splits[1], (NTX, NTY, STEPS, B, P_SIZE), 1.0, 6.0, ((0, 8), (1, 4)), jnp.float32),
        "blocks": gaussian(splits[2], (NTX, NTY, NBLK, B, B), (NBLK * B) ** -0.5, 0.09375, ((0, 8), (1, 4))),
        "self_inverse": draw_self_inverse(jax.random.fold_in(splits[6], 71), 0),
        "neighbour": plant(jax.random.randint(splits[4], (NTX, NTY, NBLK), 0, 9), jax.random.fold_in(splits[4], 1), 0, 8).astype(jnp.int32),
        "delay": plant(jax.random.randint(splits[5], (NTX, NTY, NBLK), 1, DMAX + 1), jax.random.fold_in(splits[5], 1), 1, DMAX).astype(jnp.int32),
    }


def reference(history, incident, blocks, self_inverse, neighbour, delay):
    past = jnp.flip(history, axis=2)
    padded = jnp.pad(past, ((1, 1), (1, 1), (0, 0), (0, 0), (0, 0)))
    frames = [padded]
    results = []
    columns = jnp.arange(NTY, dtype=jnp.int32)[:, None]
    for step in range(STEPS):
        stack = jnp.concatenate(frames, axis=2)
        slots = (step - delay + DMAX).astype(jnp.int32)

        def one_row(row):
            near = lax.dynamic_slice_in_dim(stack, row, 3, 0)
            ids = neighbour[row]
            sources = near[ids // 3, columns + ids % 3, slots[row]]
            field = jnp.einsum("yjab,yjbp->yap", blocks[row].astype(jnp.float32), sources.astype(jnp.float32))
            rhs = incident[row, :, step] - field
            solved = jnp.einsum("yab,ybp->yap", self_inverse[row], rhs, precision=lax.Precision.HIGHEST)
            return solved.astype(jnp.bfloat16)

        current = lax.map(one_row, jnp.arange(NTX, dtype=jnp.int32))
        results.append(current)
        frames.append(jnp.pad(current, ((1, 1), (1, 1), (0, 0), (0, 0)))[:, :, None])
    return jnp.stack(results, axis=2)
```

```python
import functools

import jax
import jax.numpy as jnp
from jax import lax
from jax.experimental import pallas as pl
from jax.experimental.pallas import tpu as pltpu
from jax.sharding import PartitionSpec as P

MESH = pl.DeviceIdType.MESH
LANES = 128
GROUP = 4
MODES = ("R", "R", "R")


LAG = 5


def order(chunks, depth):
    tokens = []
    total = chunks * depth
    for i in range(total + LAG):
        if i < total:
            tokens.append(("M", i))
        if i >= LAG:
            tokens.append(("O", i - LAG))
            if (i - LAG) >= 2 * depth - 1 and (i - LAG) % depth == depth - 1:
                tokens.append(("C", (i - LAG) // depth - 1))
    tokens.append(("C", chunks - 1))
    return tokens


def kernel(
    rows,
    cols,
    near_hbm,
    lag_hbm,
    history,
    incident,
    blocks,
    inverse,
    out,
    near_ref,
    lag_ref,
    inc,
    mats,
    inv,
    split,
    recv,
    stack,
    load_sem,
    out_sem,
    send_sem,
    recv_sem,
):
    steps, basis, ports = incident.shape
    depth = history.shape[0]
    nblk = blocks.shape[0]
    chunks = ports // LANES
    items = chunks * steps
    r = lax.axis_index("px")
    c = lax.axis_index("py")
    p = 1 - 2 * lax.rem(r, 2)
    e = 1 - 2 * lax.rem(c, 2)
    yes = r >= 0
    both = jnp.logical_and

    def inside(index, size):
        return both(index >= 0, index < size)

    has_z = inside(r - p, rows)
    has_on = inside(r + 2 * p, rows)
    has_back = inside(r - 2 * p, rows)
    has_f = inside(c - e, cols)
    mate, over = (r + p, c), (r - p, c)
    near, far = (r, c + e), (r, c - e)
    on, back = (r + 2 * p, c), (r - 2 * p, c)
    mate_far, over_far = (r + p, c - e), (r - p, c - e)
    where = {
        "own": (0, 0, yes),
        "mate": (1, 0, yes),
        "over": (-1, 0, has_z),
        "near": (0, 1, yes),
        "far": (0, -1, has_f),
        "mate_near": (1, 1, yes),
        "over_near": (-1, 1, has_z),
        "mate_far": (1, -1, has_f),
        "over_far": (-1, -1, both(has_z, has_f)),
    }

    def slot_of(name, flip_p=1, flip_e=1):
        a, b, _ = where[name]
        return 4 + 3 * a * flip_p * p + b * flip_e * e

    barrier = pltpu.get_barrier_semaphore()
    greet = (
        (has_z, over),
        (both(has_z, has_f), over_far),
        (yes, mate),
        (has_f, mate_far),
        (has_on, on),
        (has_back, back),
        (has_f, far),
        (yes, near),
    )
    count = 0
    for here, peer in greet:
        count = count + here.astype(jnp.int32)

        @pl.when(here)
        def _():
            pl.semaphore_signal(barrier, inc=1, device_id=peer, device_id_type=MESH)

    own_loads = []
    for k in range(chunks):
        own_loads.append(
            pltpu.make_async_copy(
                history.at[:, :, pl.ds(k * LANES, LANES)],
                recv.at[k, 4, pl.ds(0, depth)],
                load_sem.at[k],
            )
        )
    loads = [
        pltpu.make_async_copy(near_hbm, near_ref, load_sem.at[chunks]),
        pltpu.make_async_copy(lag_hbm, lag_ref, load_sem.at[chunks + 1]),
        pltpu.make_async_copy(blocks, mats, load_sem.at[chunks + 2]),
        pltpu.make_async_copy(inverse, inv, load_sem.at[chunks + 3]),
    ]
    for k in range(chunks):
        loads.append(
            pltpu.make_async_copy(
                incident.at[:, :, pl.ds(k * LANES, LANES)], inc.at[k], load_sem.at[chunks + 4 + k]
            )
        )
    for load in own_loads + loads:
        load.start()

    def copy(k, frame, way, source, target, flip_p, flip_e, peer):
        q = frame * chunks + k
        slot = slot_of(target, flip_p, flip_e)
        return pltpu.make_async_remote_copy(
            src_ref=recv.at[k, slot_of(source), frame],
            dst_ref=recv.at[k, slot, frame],
            send_sem=send_sem.at[q * 8 + way],
            recv_sem=recv_sem.at[q * 9 + slot],
            device_id=peer,
            device_id_type=MESH,
        )

    to_mate, to_over, to_on = (mate, -1, 1), (over, -1, 1), (on, 1, 1)
    to_near, to_far = (near, 1, -1), (far, 1, -1)
    to_mate_far, to_over_far = (mate_far, -1, -1), (over_far, -1, -1)

    def start(k, frame, messages):
        for way, here, (peer, flip_p, flip_e), source, target in messages:

            @pl.when(here)
            def _():
                copy(k, frame, way, source, target, flip_p, flip_e, peer).start()

    def landed(k, frame, name):
        @pl.when(where[name][2])
        def _():
            copy(k, frame, 0, name, name, 1, 1, near).wait_recv()

    def mode_of(k):
        return MODES[k % len(MODES)]

    def own(mode):
        messages = []
        if mode == "D":
            messages += [
                (0, has_z, to_over, "own", "over"),
                (1, both(has_z, has_f), to_over_far, "own", "over_far"),
            ]
        messages += [(2, yes, to_mate, "own", "mate")]
        if mode != "R":
            messages += [(3, has_f, to_mate_far, "own", "mate_far")]
        return messages + [(4, yes, to_near, "own", "near"), (5, has_f, to_far, "own", "far")]

    def from_mate(mode):
        messages = []
        if mode != "D":
            messages += [(0, has_on, to_on, "mate", "over")]
        messages += [(6, yes, to_near, "mate", "mate_near")]
        if mode == "R":
            messages += [(3, has_f, to_far, "mate", "mate_far")]
        return messages

    def from_mate_far(mode):
        if mode == "Y":
            return [(1, both(has_on, has_f), to_on, "mate_far", "over_far")]
        return []

    def from_over(mode):
        messages = [(7, has_z, to_near, "over", "over_near")]
        if mode == "R":
            messages += [(1, both(has_z, has_f), to_far, "over", "over_far")]
        return messages

    def after_mate(k, frame, mode):
        landed(k, frame, "mate")
        start(k, frame, from_mate(mode))
        if mode == "Y":
            landed(k, frame, "mate_far")
            start(k, frame, from_mate_far(mode))

    def after_over(k, frame, mode):
        landed(k, frame, "over")
        start(k, frame, from_over(mode))

    def keep(k, frame, name):
        @pl.when(where[name][2])
        def _():
            slot = slot_of(name)
            stack[k, slot, frame] = recv[k, slot, frame]

    def rest(k, frame, mode):
        names = ["near", "far", "mate_near", "mate_far", "over_far", "over_near"]
        if mode == "Y":
            names.remove("mate_far")
        for name in names:
            landed(k, frame, name)
        for name in where:
            keep(k, frame, name)

    def drain(k, frame, mode):
        for messages in (own(mode), from_mate(mode), from_mate_far(mode), from_over(mode)):
            for way, here, (peer, flip_p, flip_e), source, target in messages:

                @pl.when(here)
                def _():
                    copy(k, frame, way, source, target, flip_p, flip_e, peer).wait_send()

    def clear(slot):
        def zero(i, carry):
            k = i // (depth + steps - 1)
            stack[k, slot, i - k * (depth + steps - 1)] = jnp.zeros((basis, LANES), stack.dtype)
            return carry

        lax.fori_loop(0, chunks * (depth + steps - 1), zero, 0)

    for name in ("over", "over_near", "over_far", "far", "mate_far"):

        @pl.when(jnp.logical_not(where[name][2]))
        def _():
            clear(slot_of(name))

    pl.semaphore_wait(barrier, count)
    for k in range(chunks):
        own_loads[k].wait()
        for d in range(depth):
            start(k, d, own(mode_of(k)))
    for load in loads:
        load.wait()
    whole = inv[...]
    high = whole.astype(jnp.bfloat16)
    low = (whole - high.astype(jnp.float32)).astype(jnp.bfloat16)
    split[...] = jnp.concatenate([high, high, low], axis=1)

    def out_copy(k, s):
        return pltpu.make_async_copy(
            recv.at[k, 4, depth + s],
            out.at[s, :, pl.ds(pl.multiple_of(k * LANES, LANES), LANES)],
            out_sem.at[s * chunks + k],
        )

    def compute(k, s):
        field = jnp.zeros((basis, LANES), jnp.float32)
        for j in range(0, nblk, GROUP):
            sources = []
            for i in range(j, j + GROUP):
                lag = jnp.maximum(lag_ref[i], 1)
                frame = jnp.where(s < lag, lag - s - 1, depth + s - lag)
                sources.append(stack[k, near_ref[i], frame])
            field = field + jnp.dot(
                jnp.concatenate([mats[i] for i in range(j, j + GROUP)], axis=1),
                jnp.concatenate(sources, axis=0),
                preferred_element_type=jnp.float32,
            )
        rhs = inc[k, s] - field
        high = rhs.astype(jnp.bfloat16)
        low = (rhs - high.astype(jnp.float32)).astype(jnp.bfloat16)
        current = jnp.dot(
            split[...],
            jnp.concatenate([high, low, high], axis=0),
            preferred_element_type=jnp.float32,
        ).astype(jnp.bfloat16)
        recv[k, 4, depth + s] = current

        @pl.when(s + 1 < steps)
        def _():
            start(k, depth + s, own("D"))

        out_copy(k, s).start()

    for token, n in order(chunks, depth):
        k = n // depth if token in "MO" else n
        if token == "M":
            after_mate(k, n % depth, mode_of(k))
        elif token == "O":
            after_over(k, n % depth, mode_of(k))
        else:
            for d in range(depth):
                rest(k, d, mode_of(k))
            compute(k, jnp.int32(0))

    def body(q, carry):
        s = q // chunks
        k = q - s * chunks
        after_mate(k, depth + s - 1, "D")
        after_over(k, depth + s - 1, "D")
        rest(k, depth + s - 1, "D")
        compute(k, s)
        return carry

    lax.fori_loop(chunks, items, body, 0)

    for k in range(chunks):

        def settle(d, carry):
            drain(k, d, mode_of(k))
            return carry

        lax.fori_loop(0, depth, settle, 0)

    def finish(q, carry):
        s = q // chunks
        k = q - s * chunks
        out_copy(k, s).wait()

        @pl.when(s + 1 < steps)
        def _():
            drain(k, depth + s, "D")

        return carry

    lax.fori_loop(0, items, finish, 0)


def local(rows, cols, history, incident, blocks, self_inverse, neighbour, delay):
    depth, basis, ports = history.shape[2:]
    steps = incident.shape[2]
    nblk = blocks.shape[2]
    chunks = ports // LANES
    items = chunks * steps
    hbm = pl.BlockSpec(memory_space=pl.ANY)
    half = jnp.bfloat16
    currents = pl.pallas_call(
        functools.partial(kernel, rows, cols),
        out_shape=jax.ShapeDtypeStruct((steps, basis, ports), half),
        in_specs=[hbm] * 6,
        out_specs=hbm,
        scratch_shapes=[
            pltpu.SMEM((nblk,), jnp.int32),
            pltpu.SMEM((nblk,), jnp.int32),
            pltpu.VMEM((chunks, steps, basis, LANES), jnp.float32),
            pltpu.VMEM((nblk, basis, basis), half),
            pltpu.VMEM((basis, basis), jnp.float32),
            pltpu.VMEM((basis, 3 * basis), half),
            pltpu.VMEM((chunks, 9, depth + steps, basis, LANES), half),
            pltpu.VMEM((chunks, 9, depth + steps - 1, basis, LANES), half),
            pltpu.SemaphoreType.DMA((2 * chunks + 4,)),
            pltpu.SemaphoreType.DMA((items,)),
            pltpu.SemaphoreType.DMA((chunks * (depth + steps - 1) * 8,)),
            pltpu.SemaphoreType.DMA((chunks * (depth + steps - 1) * 9,)),
        ],
        compiler_params=pltpu.CompilerParams(
            collective_id=0, has_side_effects=True, vmem_limit_bytes=63 * 1024 * 1024
        ),
    )(
        neighbour[0, 0],
        delay[0, 0],
        history[0, 0],
        incident[0, 0],
        blocks[0, 0],
        self_inverse[0, 0],
    )
    return currents[None, None]


def solution(mesh):
    in_specs = (
        P("px", "py", None, None, None),
        P("px", "py", None, None, None),
        P("px", "py", None, None, None),
        P("px", "py", None, None),
        P("px", "py", None),
        P("px", "py", None),
    )
    out_specs = P("px", "py", None, None, None)
    body = functools.partial(local, mesh.shape["px"], mesh.shape["py"])
    return jax.shard_map(body, mesh=mesh, in_specs=in_specs, out_specs=out_specs, check_vma=False)
```

```python
import functools

import jax
import jax.numpy as jnp
from jax import lax
from jax.experimental import pallas as pl
from jax.experimental.pallas import tpu as pltpu
from jax.sharding import PartitionSpec as P

MESH = pl.DeviceIdType.MESH
LANES = 128
GROUP = 4
PAST = "RXX"
NEXT = "DDD"


LAG = 4


def kernel(
    rows,
    cols,
    near_hbm,
    lag_hbm,
    history,
    incident,
    blocks,
    inverse,
    out,
    near_ref,
    lag_ref,
    inc,
    mats,
    inv,
    split,
    recv,
    stack,
    load_sem,
    out_sem,
    send_sem,
    recv_sem,
):
    steps, basis, ports = incident.shape
    depth = history.shape[0]
    nblk = blocks.shape[0]
    chunks = ports // LANES
    items = chunks * steps
    r = lax.axis_index("px")
    c = lax.axis_index("py")
    p = 1 - 2 * lax.rem(r, 2)
    e = 1 - 2 * lax.rem(c, 2)
    yes = r >= 0
    both = jnp.logical_and

    def inside(index, size):
        return both(index >= 0, index < size)

    has_z = inside(r - p, rows)
    has_on = inside(r + 2 * p, rows)
    has_back = inside(r - 2 * p, rows)
    has_f = inside(c - e, cols)
    mate, over = (r + p, c), (r - p, c)
    near, far = (r, c + e), (r, c - e)
    on, back = (r + 2 * p, c), (r - 2 * p, c)
    mate_far, over_far = (r + p, c - e), (r - p, c - e)
    where = {
        "own": (0, 0, yes),
        "mate": (1, 0, yes),
        "over": (-1, 0, has_z),
        "near": (0, 1, yes),
        "far": (0, -1, has_f),
        "mate_near": (1, 1, yes),
        "over_near": (-1, 1, has_z),
        "mate_far": (1, -1, has_f),
        "over_far": (-1, -1, both(has_z, has_f)),
    }

    def slot_of(name, flip_p=1, flip_e=1):
        a, b, _ = where[name]
        return 4 + 3 * a * flip_p * p + b * flip_e * e

    barrier = pltpu.get_barrier_semaphore()
    greet = (
        (has_z, over),
        (both(has_z, has_f), over_far),
        (yes, mate),
        (has_f, mate_far),
        (has_on, on),
        (has_back, back),
        (has_f, far),
        (yes, near),
    )
    count = 0
    for here, peer in greet:
        count = count + here.astype(jnp.int32)

        @pl.when(here)
        def _():
            pl.semaphore_signal(barrier, inc=1, device_id=peer, device_id_type=MESH)

    own_loads = []
    for k in range(chunks):
        own_loads.append(
            pltpu.make_async_copy(
                history.at[:, :, pl.ds(k * LANES, LANES)],
                recv.at[k, 4, pl.ds(0, depth)],
                load_sem.at[k],
            )
        )
    loads = [
        pltpu.make_async_copy(near_hbm, near_ref, load_sem.at[chunks]),
        pltpu.make_async_copy(lag_hbm, lag_ref, load_sem.at[chunks + 1]),
        pltpu.make_async_copy(blocks, mats, load_sem.at[chunks + 2]),
        pltpu.make_async_copy(inverse, inv, load_sem.at[chunks + 3]),
    ]
    for k in range(chunks):
        loads.append(
            pltpu.make_async_copy(
                incident.at[:, :, pl.ds(k * LANES, LANES)], inc.at[k], load_sem.at[chunks + 4 + k]
            )
        )
    for load in own_loads + loads:
        load.start()

    def copy(k, frame, way, source, target, flip_p, flip_e, peer):
        q = frame * chunks + k
        slot = slot_of(target, flip_p, flip_e)
        return pltpu.make_async_remote_copy(
            src_ref=recv.at[k, slot_of(source), frame],
            dst_ref=recv.at[k, slot, frame],
            send_sem=send_sem.at[q * 8 + way],
            recv_sem=recv_sem.at[q * 9 + slot],
            device_id=peer,
            device_id_type=MESH,
        )

    to_mate, to_over, to_on = (mate, -1, 1), (over, -1, 1), (on, 1, 1)
    to_near, to_far = (near, 1, -1), (far, 1, -1)
    to_mate_far, to_over_far = (mate_far, -1, -1), (over_far, -1, -1)

    def start(k, frame, messages):
        for way, here, (peer, flip_p, flip_e), source, target in messages:

            @pl.when(here)
            def _():
                copy(k, frame, way, source, target, flip_p, flip_e, peer).start()

    def landed(k, frame, name):
        @pl.when(where[name][2])
        def _():
            copy(k, frame, 0, name, name, 1, 1, near).wait_recv()

    def own(mode):
        messages = []
        if mode[0] == "D":
            messages += [(0, has_z, to_over, "own", "over")]
        if mode[2] == "D":
            messages += [(1, both(has_z, has_f), to_over_far, "own", "over_far")]
        messages += [(2, yes, to_mate, "own", "mate")]
        if mode[1] == "D":
            messages += [(3, has_f, to_mate_far, "own", "mate_far")]
        return messages + [(4, yes, to_near, "own", "near"), (5, has_f, to_far, "own", "far")]

    def from_mate(mode):
        messages = []
        if mode[0] == "R":
            messages += [(0, has_on, to_on, "mate", "over")]
        if mode[1] == "X":
            messages += [(3, has_f, to_far, "mate", "mate_far")]
        return messages + [(6, yes, to_near, "mate", "mate_near")]

    def from_mate_far(mode):
        if mode[2] == "R":
            return [(1, both(has_on, has_f), to_on, "mate_far", "over_far")]
        return []

    def from_over(mode):
        messages = []
        if mode[2] == "X":
            messages += [(1, both(has_z, has_f), to_far, "over", "over_far")]
        return messages + [(7, has_z, to_near, "over", "over_near")]

    def after_mate(k, frame, mode):
        landed(k, frame, "mate")
        start(k, frame, from_mate(mode))
        if mode[2] == "R":
            landed(k, frame, "mate_far")
            start(k, frame, from_mate_far(mode))
        keep(k, frame, "mate")

    def after_over(k, frame, mode):
        landed(k, frame, "over")
        start(k, frame, from_over(mode))
        keep(k, frame, "over")

    def keep(k, frame, name):
        @pl.when(where[name][2])
        def _():
            slot = slot_of(name)
            stack[k, slot, frame] = recv[k, slot, frame]

    def rest(k, frame, mode):
        names = ["near", "far", "mate_near", "mate_far", "over_far", "over_near"]
        if mode[2] == "R":
            names.remove("mate_far")
        keep(k, frame, "own")
        for name in names:
            landed(k, frame, name)
            keep(k, frame, name)

    def drain(k, frame, mode):
        for messages in (own(mode), from_mate(mode), from_mate_far(mode), from_over(mode)):
            for way, here, (peer, flip_p, flip_e), source, target in messages:

                @pl.when(here)
                def _():
                    copy(k, frame, way, source, target, flip_p, flip_e, peer).wait_send()

    def clear(slot):
        def zero(i, carry):
            k = i // (depth + steps - 1)
            stack[k, slot, i - k * (depth + steps - 1)] = jnp.zeros((basis, LANES), stack.dtype)
            return carry

        lax.fori_loop(0, chunks * (depth + steps - 1), zero, 0)

    for name in ("over", "over_near", "over_far", "far", "mate_far"):

        @pl.when(jnp.logical_not(where[name][2]))
        def _():
            clear(slot_of(name))

    pl.semaphore_wait(barrier, count)
    for k in range(chunks):
        own_loads[k].wait()
        for d in range(depth):
            start(k, d, own(PAST))
    for load in loads:
        load.wait()
    whole = inv[...]
    high = whole.astype(jnp.bfloat16)
    low = (whole - high.astype(jnp.float32)).astype(jnp.bfloat16)
    split[...] = jnp.concatenate([high, high, low], axis=1)

    def out_copy(k, s):
        return pltpu.make_async_copy(
            recv.at[k, 4, depth + s],
            out.at[s, :, pl.ds(pl.multiple_of(k * LANES, LANES), LANES)],
            out_sem.at[s * chunks + k],
        )

    def compute(k, s):
        field = jnp.zeros((basis, LANES), jnp.float32)
        for j in range(0, nblk, GROUP):
            sources = []
            for i in range(j, j + GROUP):
                lag = jnp.maximum(lag_ref[i], 1)
                frame = jnp.where(s < lag, lag - s - 1, depth + s - lag)
                sources.append(stack[k, near_ref[i], frame])
            field = field + jnp.dot(
                jnp.concatenate([mats[i] for i in range(j, j + GROUP)], axis=1),
                jnp.concatenate(sources, axis=0),
                preferred_element_type=jnp.float32,
            )
        rhs = inc[k, s] - field
        high = rhs.astype(jnp.bfloat16)
        low = (rhs - high.astype(jnp.float32)).astype(jnp.bfloat16)
        current = jnp.dot(
            split[...],
            jnp.concatenate([high, low, high], axis=0),
            preferred_element_type=jnp.float32,
        ).astype(jnp.bfloat16)
        recv[k, 4, depth + s] = current

        @pl.when(s + 1 < steps)
        def _():
            start(k, depth + s, own(NEXT))

        out_copy(k, s).start()

    pieces = chunks * depth
    lead = pieces + LAG

    def piece(i):
        k = i // depth
        return k, i - k * depth

    def body(t, carry):
        @pl.when(t < pieces)
        def _():
            k, d = piece(t)
            after_mate(k, d, PAST)

        @pl.when(both(t >= LAG, t < lead))
        def _():
            k, d = piece(t - LAG)
            after_over(k, d, PAST)

        old = t - LAG
        q = jnp.where(t < lead, old // depth - 1, t - lead + chunks - 1)
        s = q // chunks
        k = q - s * chunks

        @pl.when(t > lead)
        def _():
            after_over(k, depth + s - 1, NEXT)
            after_mate(k, depth + s - 1, NEXT)
            rest(k, depth + s - 1, NEXT)

        ready = both(old >= 2 * depth - 1, lax.rem(old + depth, depth) == depth - 1)

        @pl.when(both(t <= lead, jnp.logical_or(t == lead, ready)))
        def _():
            for d in range(depth):
                rest(k, d, PAST)

        @pl.when(jnp.logical_or(t >= lead, ready))
        def _():
            compute(k, s)

        return carry

    lax.fori_loop(0, lead + items - chunks + 1, body, 0)

    def finish(q, carry):
        s = q // chunks
        k = q - s * chunks
        out_copy(k, s).wait()

        @pl.when(s + 1 < steps)
        def _():
            drain(k, depth + s, NEXT)

        return carry

    def settle(i, carry):
        k, d = piece(i)
        drain(k, d, PAST)
        return carry

    lax.fori_loop(0, pieces, settle, 0)
    lax.fori_loop(0, items, finish, 0)


def local(rows, cols, history, incident, blocks, self_inverse, neighbour, delay):
    depth, basis, ports = history.shape[2:]
    steps = incident.shape[2]
    nblk = blocks.shape[2]
    chunks = ports // LANES
    items = chunks * steps
    hbm = pl.BlockSpec(memory_space=pl.ANY)
    half = jnp.bfloat16
    currents = pl.pallas_call(
        functools.partial(kernel, rows, cols),
        out_shape=jax.ShapeDtypeStruct((steps, basis, ports), half),
        in_specs=[hbm] * 6,
        out_specs=hbm,
        scratch_shapes=[
            pltpu.SMEM((nblk,), jnp.int32),
            pltpu.SMEM((nblk,), jnp.int32),
            pltpu.VMEM((chunks, steps, basis, LANES), jnp.float32),
            pltpu.VMEM((nblk, basis, basis), half),
            pltpu.VMEM((basis, basis), jnp.float32),
            pltpu.VMEM((basis, 3 * basis), half),
            pltpu.VMEM((chunks, 9, depth + steps, basis, LANES), half),
            pltpu.VMEM((chunks, 9, depth + steps - 1, basis, LANES), half),
            pltpu.SemaphoreType.DMA((2 * chunks + 4,)),
            pltpu.SemaphoreType.DMA((items,)),
            pltpu.SemaphoreType.DMA((chunks * (depth + steps - 1) * 8,)),
            pltpu.SemaphoreType.DMA((chunks * (depth + steps - 1) * 9,)),
        ],
        compiler_params=pltpu.CompilerParams(
            collective_id=0, has_side_effects=True, vmem_limit_bytes=63 * 1024 * 1024
        ),
    )(
        neighbour[0, 0],
        delay[0, 0],
        history[0, 0],
        incident[0, 0],
        blocks[0, 0],
        self_inverse[0, 0],
    )
    return currents[None, None]


def solution(mesh):
    in_specs = (
        P("px", "py", None, None, None),
        P("px", "py", None, None, None),
        P("px", "py", None, None, None),
        P("px", "py", None, None),
        P("px", "py", None),
        P("px", "py", None),
    )
    out_specs = P("px", "py", None, None, None)
    body = functools.partial(local, mesh.shape["px"], mesh.shape["py"])
    return jax.shard_map(body, mesh=mesh, in_specs=in_specs, out_specs=out_specs, check_vma=False)
```

```python
import functools

import jax
import jax.numpy as jnp
from jax import lax
from jax.experimental import pallas as pl
from jax.experimental.pallas import tpu as pltpu
from jax.sharding import PartitionSpec as P

MESH = pl.DeviceIdType.MESH
LANES = 128
GROUP = 16
PAST = "RXX"
NEXT = "DDD"


LAG = 4
HOLD = 3
HALVES = 2


def kernel(
    rows,
    cols,
    near_hbm,
    lag_hbm,
    history,
    incident,
    blocks,
    inverse,
    *others,
):
    steps, basis, ports = incident.shape
    outs = others[: HALVES * steps]
    (near_ref, lag_ref, place, inc, mats, inv, split, recv, stack, load_sem, out_sem, send_sem, recv_sem) = others[
        HALVES * steps :
    ]
    depth = history.shape[0]
    nblk = blocks.shape[0]
    chunks = ports // LANES
    items = chunks * steps
    frames = depth + steps - 1
    r = lax.axis_index("px")
    c = lax.axis_index("py")
    p = 1 - 2 * lax.rem(r, 2)
    e = 1 - 2 * lax.rem(c, 2)
    yes = r >= 0
    both = jnp.logical_and

    def inside(index, size):
        return both(index >= 0, index < size)

    has_z = inside(r - p, rows)
    has_on = inside(r + 2 * p, rows)
    has_back = inside(r - 2 * p, rows)
    has_f = inside(c - e, cols)
    mate, over = (r + p, c), (r - p, c)
    near, far = (r, c + e), (r, c - e)
    on, back = (r + 2 * p, c), (r - 2 * p, c)
    mate_far, over_far = (r + p, c - e), (r - p, c - e)
    where = {
        "own": (0, 0, yes),
        "mate": (1, 0, yes),
        "over": (-1, 0, has_z),
        "near": (0, 1, yes),
        "far": (0, -1, has_f),
        "mate_near": (1, 1, yes),
        "over_near": (-1, 1, has_z),
        "mate_far": (1, -1, has_f),
        "over_far": (-1, -1, both(has_z, has_f)),
    }

    def slot_of(name, flip_p=1, flip_e=1):
        a, b, _ = where[name]
        return 4 + 3 * a * flip_p * p + b * flip_e * e

    barrier = pltpu.get_barrier_semaphore()
    greet = (
        (has_z, over),
        (both(has_z, has_f), over_far),
        (yes, mate),
        (has_f, mate_far),
        (has_on, on),
        (has_back, back),
        (has_f, far),
        (yes, near),
    )
    count = 0
    for here, peer in greet:
        count = count + here.astype(jnp.int32)

        @pl.when(here)
        def _():
            pl.semaphore_signal(barrier, inc=1, device_id=peer, device_id_type=MESH)

    own_loads = [
        [
            pltpu.make_async_copy(
                history.at[depth - 1 - d, :, pl.ds(k * LANES, LANES)],
                recv.at[k, 4, d],
                load_sem.at[k * depth + d],
            )
            for d in range(depth)
        ]
        for k in range(chunks)
    ]
    loads = [
        pltpu.make_async_copy(near_hbm, near_ref, load_sem.at[chunks * depth]),
        pltpu.make_async_copy(lag_hbm, lag_ref, load_sem.at[chunks * depth + 1]),
        pltpu.make_async_copy(blocks, mats, load_sem.at[chunks * depth + 2]),
        pltpu.make_async_copy(inverse, inv, load_sem.at[chunks * depth + 3]),
    ]
    for k in range(chunks):
        loads.append(
            pltpu.make_async_copy(
                incident.at[:, :, pl.ds(k * LANES, LANES)], inc.at[k], load_sem.at[chunks * depth + 4 + k]
            )
        )
    for load in sum(own_loads, []) + loads:
        load.start()

    def copy(k, frame, way, source, target, flip_p, flip_e, peer):
        q = frame * chunks + k
        slot = slot_of(target, flip_p, flip_e)
        return pltpu.make_async_remote_copy(
            src_ref=recv.at[k, slot_of(source), frame],
            dst_ref=recv.at[k, slot, frame],
            send_sem=send_sem.at[q * 8 + way],
            recv_sem=recv_sem.at[q * 9 + slot],
            device_id=peer,
            device_id_type=MESH,
        )

    to_mate, to_over, to_on = (mate, -1, 1), (over, -1, 1), (on, 1, 1)
    to_near, to_far = (near, 1, -1), (far, 1, -1)
    to_mate_far, to_over_far = (mate_far, -1, -1), (over_far, -1, -1)

    def start(k, frame, messages):
        for way, here, (peer, flip_p, flip_e), source, target in messages:

            @pl.when(here)
            def _():
                copy(k, frame, way, source, target, flip_p, flip_e, peer).start()

    def landed(k, frame, name):
        @pl.when(where[name][2])
        def _():
            copy(k, frame, 0, name, name, 1, 1, near).wait_recv()

    def own(mode):
        messages = []
        if mode[0] == "D":
            messages += [(0, has_z, to_over, "own", "over")]
        if mode[2] == "D":
            messages += [(1, both(has_z, has_f), to_over_far, "own", "over_far")]
        messages += [(2, yes, to_mate, "own", "mate")]
        if mode[1] == "D":
            messages += [(3, has_f, to_mate_far, "own", "mate_far")]
        return messages + [(4, yes, to_near, "own", "near"), (5, has_f, to_far, "own", "far")]

    def from_mate(mode):
        messages = []
        if mode[0] == "R":
            messages += [(0, has_on, to_on, "mate", "over")]
        if mode[1] == "X":
            messages += [(3, has_f, to_far, "mate", "mate_far")]
        return messages + [(6, yes, to_near, "mate", "mate_near")]

    def from_mate_far(mode):
        if mode[2] == "R":
            return [(1, both(has_on, has_f), to_on, "mate_far", "over_far")]
        return []

    def from_over(mode):
        messages = []
        if mode[2] == "X":
            messages += [(1, both(has_z, has_f), to_far, "over", "over_far")]
        return messages + [(7, has_z, to_near, "over", "over_near")]

    def after_mate(k, frame, mode):
        landed(k, frame, "mate")
        start(k, frame, from_mate(mode))
        if mode[2] == "R":
            landed(k, frame, "mate_far")
            start(k, frame, from_mate_far(mode))
        keep(k, frame, "mate")

    def after_over(k, frame, mode):
        landed(k, frame, "over")
        start(k, frame, from_over(mode))
        keep(k, frame, "over")

    def keep(k, frame, name):
        @pl.when(where[name][2])
        def _():
            slot = slot_of(name)
            stack[(k * 9 + slot) * frames + frame] = recv[k, slot, frame]

    def rest(k, frame, mode):
        names = ["near", "far", "mate_far", "over_far", "over_near", "mate_near"]
        if mode[2] == "R":
            names.remove("mate_far")
        for name in names:
            landed(k, frame, name)
            keep(k, frame, name)

    def drain(k, frame, mode):
        for messages in (own(mode), from_mate(mode), from_mate_far(mode), from_over(mode)):
            for way, here, (peer, flip_p, flip_e), source, target in messages:

                @pl.when(here)
                def _():
                    copy(k, frame, way, source, target, flip_p, flip_e, peer).wait_send()

    def clear(slot):
        def zero(i, carry):
            k = i // frames
            stack[(k * 9 + slot) * frames + i - k * frames] = jnp.zeros((basis, LANES), stack.dtype)
            return carry

        lax.fori_loop(0, chunks * frames, zero, 0)

    for name in ("over", "over_near", "over_far", "far", "mate_far"):

        @pl.when(jnp.logical_not(where[name][2]))
        def _():
            clear(slot_of(name))

    pl.semaphore_wait(barrier, count)
    for k in range(chunks):
        for d in range(depth):
            own_loads[k][d].wait()
            start(k, d, own(PAST))
    for k in range(chunks):
        for d in range(depth):
            keep(k, d, "own")
    for load in loads:
        load.wait()
    whole = inv[...]
    high = whole.astype(jnp.bfloat16)
    low = (whole - high.astype(jnp.float32)).astype(jnp.bfloat16)
    split[...] = jnp.concatenate([high, high, low], axis=1)

    for i in range(nblk):
        place[i] = near_ref[i] * frames + depth - jnp.maximum(lag_ref[i], 1)

    def out_copies(k, step):
        lanes = pl.ds(pl.multiple_of(k * LANES, LANES), LANES)
        part = basis // HALVES
        return [
            pltpu.make_async_copy(
                recv.at[k, 4, depth + step, pl.ds(h * part, part)],
                outs[step * HALVES + h].at[:, lanes],
                out_sem.at[(step * chunks + k) * HALVES + h],
            )
            for h in range(HALVES)
        ]

    def each_step(s, act):
        for step in range(steps):

            @pl.when(s == step)
            def _():
                act(step)

    def write(k, step):
        for move in out_copies(k, step):
            move.start()

    def written(k, step):
        for move in out_copies(k, step):
            move.wait()

    def compute(k, s):
        first = k * 9 * frames + s
        field = jnp.zeros((basis, LANES), jnp.float32)
        for j in range(0, nblk, GROUP):
            sources = []
            for i in range(j, j + GROUP):
                sources.append(stack[first + place[i]])
            field = field + jnp.dot(
                jnp.concatenate([mats[i] for i in range(j, j + GROUP)], axis=1),
                jnp.concatenate(sources, axis=0),
                preferred_element_type=jnp.float32,
            )
        rhs = inc[k, s] - field
        high = rhs.astype(jnp.bfloat16)
        low = (rhs - high.astype(jnp.float32)).astype(jnp.bfloat16)
        current = jnp.dot(
            split[...],
            jnp.concatenate([high, low, high], axis=0),
            preferred_element_type=jnp.float32,
        ).astype(jnp.bfloat16)
        recv[k, 4, depth + s] = current

        @pl.when(s + 1 < steps)
        def _():
            stack[(k * 9 + 4) * frames + depth + s] = current

        @pl.when(s + 1 < steps)
        def _():
            start(k, depth + s, own(NEXT))

        @pl.when(s == steps - 1)
        def _():
            write(k, steps - 1)

    pieces = chunks * depth
    last = LAG + HOLD + pieces - 1

    def piece(i):
        k = i // depth
        return k, i - k * depth

    def body(t, carry):
        @pl.when(t < pieces)
        def _():
            k, d = piece(t)
            after_mate(k, d, PAST)

        @pl.when(both(t >= LAG, t < LAG + pieces))
        def _():
            k, d = piece(t - LAG)
            after_over(k, d, PAST)

        whole = t - LAG - HOLD + 1
        first = t <= last
        q = jnp.where(first, whole // depth - 1, t - last + chunks - 1)
        s = q // chunks
        k = q - s * chunks

        @pl.when(jnp.logical_not(first))
        def _():
            after_over(k, depth + s - 1, NEXT)
            after_mate(k, depth + s - 1, NEXT)
            @pl.when(q < chunks + pieces)
            def _():
                past_k, past_d = piece(q - chunks)
                drain(past_k, past_d, PAST)

            @pl.when(s >= 2)
            def _():
                drain(k, depth + s - 2, NEXT)

            each_step(s - 1, lambda step: write(k, step))
            each_step(s - 2, lambda step: written(k, step))
            rest(k, depth + s - 1, NEXT)

        ready = both(whole >= depth, lax.rem(whole, depth) == 0)

        @pl.when(both(first, ready))
        def _():
            for d in range(depth):
                rest(k, d, PAST)

        @pl.when(jnp.logical_or(jnp.logical_not(first), ready))
        def _():
            compute(k, s)

        return carry

    lax.fori_loop(0, last + 1 + items - chunks, body, 0)

    def settle(i, carry):
        k, d = piece(i)
        drain(k, d, PAST)
        return carry

    lax.fori_loop(items - chunks, pieces, settle, 0)

    def finish(k, carry):
        drain(k, depth + steps - 2, NEXT)
        written(k, steps - 2)
        written(k, steps - 1)
        return carry

    lax.fori_loop(0, chunks, finish, 0)


def local(rows, cols, history, incident, blocks, self_inverse, neighbour, delay):
    depth, basis, ports = history.shape[2:]
    steps = incident.shape[2]
    nblk = blocks.shape[2]
    chunks = ports // LANES
    items = chunks * steps
    hbm = pl.BlockSpec(memory_space=pl.ANY)
    half = jnp.bfloat16
    currents = pl.pallas_call(
        functools.partial(kernel, rows, cols),
        out_shape=[jax.ShapeDtypeStruct((basis // HALVES, ports), half)] * (steps * HALVES),
        in_specs=[hbm] * 6,
        out_specs=[hbm] * (steps * HALVES),
        scratch_shapes=[
            pltpu.SMEM((nblk,), jnp.int32),
            pltpu.SMEM((nblk,), jnp.int32),
            pltpu.SMEM((nblk,), jnp.int32),
            pltpu.VMEM((chunks, steps, basis, LANES), jnp.float32),
            pltpu.VMEM((nblk, basis, basis), half),
            pltpu.VMEM((basis, basis), jnp.float32),
            pltpu.VMEM((basis, 3 * basis), half),
            pltpu.VMEM((chunks, 9, depth + steps, basis, LANES), half),
            pltpu.VMEM((chunks * 9 * (depth + steps - 1), basis, LANES), half),
            pltpu.SemaphoreType.DMA((chunks * depth + chunks + 4,)),
            pltpu.SemaphoreType.DMA((items * HALVES,)),
            pltpu.SemaphoreType.DMA((chunks * (depth + steps - 1) * 8,)),
            pltpu.SemaphoreType.DMA((chunks * (depth + steps - 1) * 9,)),
        ],
        compiler_params=pltpu.CompilerParams(
            collective_id=0, has_side_effects=True, vmem_limit_bytes=107 * 512 * 1024
        ),
    )(
        neighbour[0, 0],
        delay[0, 0],
        history[0, 0],
        incident[0, 0],
        blocks[0, 0],
        self_inverse[0, 0],
    )
    part = basis // HALVES

    def lay(*refs):
        whole, sem = refs[-2:]
        moves = []
        for i, ref in enumerate(refs[:-2]):
            place = whole.at[i // HALVES, pl.ds(i % HALVES * part, part)]
            moves.append(pltpu.make_async_copy(ref, place, sem.at[i]))
        for move in moves:
            move.start()
        for move in moves:
            move.wait()

    whole = pl.pallas_call(
        lay,
        out_shape=jax.ShapeDtypeStruct((steps, basis, ports), half),
        in_specs=[hbm] * len(currents),
        out_specs=hbm,
        scratch_shapes=[pltpu.SemaphoreType.DMA((len(currents),))],
        compiler_params=pltpu.CompilerParams(vmem_limit_bytes=1024 * 1024),
    )(*currents)
    return whole[None, None]


def solution(mesh):
    in_specs = (
        P("px", "py", None, None, None),
        P("px", "py", None, None, None),
        P("px", "py", None, None, None),
        P("px", "py", None, None),
        P("px", "py", None),
        P("px", "py", None),
    )
    out_specs = P("px", "py", None, None, None)
    body = functools.partial(local, mesh.shape["px"], mesh.shape["py"])
    return jax.shard_map(body, mesh=mesh, in_specs=in_specs, out_specs=out_specs, check_vma=False)
```

```python
import functools

import jax
import jax.numpy as jnp
from jax import lax
from jax.experimental import pallas as pl
from jax.experimental.pallas import tpu as pltpu
from jax.sharding import PartitionSpec as P

MESH = pl.DeviceIdType.MESH
LANES = 128
GROUP = 16
PAST = "RXX"
NEXT = "DDD"


LAG = 4
HOLD = 3
AHEAD = 5
HALVES = 2


def kernel(
    rows,
    cols,
    near_hbm,
    lag_hbm,
    history,
    incident,
    blocks,
    inverse,
    *others,
):
    steps, basis, ports = incident.shape
    outs = others[: HALVES * steps]
    (near_ref, lag_ref, place, inc, mats, inv, split, recv, stack, load_sem, out_sem, send_sem, recv_sem) = others[
        HALVES * steps :
    ]
    depth = history.shape[0]
    nblk = blocks.shape[0]
    chunks = ports // LANES
    items = chunks * steps
    frames = depth + steps - 1
    r = lax.axis_index("px")
    c = lax.axis_index("py")
    p = 1 - 2 * lax.rem(r, 2)
    e = 1 - 2 * lax.rem(c, 2)
    yes = r >= 0
    both = jnp.logical_and

    def inside(index, size):
        return both(index >= 0, index < size)

    has_z = inside(r - p, rows)
    has_on = inside(r + 2 * p, rows)
    has_back = inside(r - 2 * p, rows)
    has_f = inside(c - e, cols)
    mate, over = (r + p, c), (r - p, c)
    near, far = (r, c + e), (r, c - e)
    on, back = (r + 2 * p, c), (r - 2 * p, c)
    mate_far, over_far = (r + p, c - e), (r - p, c - e)
    where = {
        "own": (0, 0, yes),
        "mate": (1, 0, yes),
        "over": (-1, 0, has_z),
        "near": (0, 1, yes),
        "far": (0, -1, has_f),
        "mate_near": (1, 1, yes),
        "over_near": (-1, 1, has_z),
        "mate_far": (1, -1, has_f),
        "over_far": (-1, -1, both(has_z, has_f)),
    }

    def slot_of(name, flip_p=1, flip_e=1):
        a, b, _ = where[name]
        return 4 + 3 * a * flip_p * p + b * flip_e * e

    barrier = pltpu.get_barrier_semaphore()
    greet = (
        (has_z, over),
        (both(has_z, has_f), over_far),
        (yes, mate),
        (has_f, mate_far),
        (has_on, on),
        (has_back, back),
        (has_f, far),
        (yes, near),
    )
    count = 0
    for here, peer in greet:
        count = count + here.astype(jnp.int32)

        @pl.when(here)
        def _():
            pl.semaphore_signal(barrier, inc=1, device_id=peer, device_id_type=MESH)

    own_loads = [
        [
            pltpu.make_async_copy(
                history.at[depth - 1 - d, :, pl.ds(k * LANES, LANES)],
                recv.at[k, 4, d],
                load_sem.at[k * depth + d],
            )
            for d in range(depth)
        ]
        for k in range(chunks)
    ]
    loads = [
        pltpu.make_async_copy(near_hbm, near_ref, load_sem.at[chunks * depth]),
        pltpu.make_async_copy(lag_hbm, lag_ref, load_sem.at[chunks * depth + 1]),
        pltpu.make_async_copy(blocks, mats, load_sem.at[chunks * depth + 2]),
        pltpu.make_async_copy(inverse, inv, load_sem.at[chunks * depth + 3]),
    ]
    for k in range(chunks):
        loads.append(
            pltpu.make_async_copy(
                incident.at[:, :, pl.ds(k * LANES, LANES)], inc.at[k], load_sem.at[chunks * depth + 4 + k]
            )
        )
    for load in sum(own_loads, []) + loads:
        load.start()

    def copy(k, frame, way, source, target, flip_p, flip_e, peer):
        q = frame * chunks + k
        slot = slot_of(target, flip_p, flip_e)
        return pltpu.make_async_remote_copy(
            src_ref=recv.at[k, slot_of(source), frame],
            dst_ref=recv.at[k, slot, frame],
            send_sem=send_sem.at[q * 8 + way],
            recv_sem=recv_sem.at[q * 9 + slot],
            device_id=peer,
            device_id_type=MESH,
        )

    to_mate, to_over, to_on = (mate, -1, 1), (over, -1, 1), (on, 1, 1)
    to_near, to_far = (near, 1, -1), (far, 1, -1)
    to_mate_far, to_over_far = (mate_far, -1, -1), (over_far, -1, -1)

    def start(k, frame, messages):
        for way, here, (peer, flip_p, flip_e), source, target in messages:

            @pl.when(here)
            def _():
                copy(k, frame, way, source, target, flip_p, flip_e, peer).start()

    def landed(k, frame, name):
        @pl.when(where[name][2])
        def _():
            copy(k, frame, 0, name, name, 1, 1, near).wait_recv()

    def own(mode):
        messages = []
        if mode[0] == "D":
            messages += [(0, has_z, to_over, "own", "over")]
        if mode[2] == "D":
            messages += [(1, both(has_z, has_f), to_over_far, "own", "over_far")]
        messages += [(2, yes, to_mate, "own", "mate")]
        if mode[1] == "D":
            messages += [(3, has_f, to_mate_far, "own", "mate_far")]
        return messages + [(4, yes, to_near, "own", "near"), (5, has_f, to_far, "own", "far")]

    def from_mate(mode):
        messages = []
        if mode[0] == "R":
            messages += [(0, has_on, to_on, "mate", "over")]
        if mode[1] == "X":
            messages += [(3, has_f, to_far, "mate", "mate_far")]
        return messages + [(6, yes, to_near, "mate", "mate_near")]

    def from_mate_far(mode):
        if mode[2] == "R":
            return [(1, both(has_on, has_f), to_on, "mate_far", "over_far")]
        return []

    def from_over(mode):
        messages = []
        if mode[2] == "X":
            messages += [(1, both(has_z, has_f), to_far, "over", "over_far")]
        return messages + [(7, has_z, to_near, "over", "over_near")]

    def after_mate(k, frame, mode):
        landed(k, frame, "mate")
        start(k, frame, from_mate(mode))
        if mode[2] == "R":
            landed(k, frame, "mate_far")
            start(k, frame, from_mate_far(mode))
        keep(k, frame, "mate")

    def after_over(k, frame, mode):
        landed(k, frame, "over")
        start(k, frame, from_over(mode))
        keep(k, frame, "over")

    def keep(k, frame, name):
        @pl.when(where[name][2])
        def _():
            slot = slot_of(name)
            stack[(k * 9 + slot) * frames + frame] = recv[k, slot, frame]

    def rest(k, frame, mode):
        names = ["near", "far", "mate_far", "over_far", "over_near", "mate_near"]
        if mode[2] == "R":
            names.remove("mate_far")
        for name in names:
            landed(k, frame, name)
            keep(k, frame, name)

    def drain(k, frame, mode):
        for messages in (own(mode), from_mate(mode), from_mate_far(mode), from_over(mode)):
            for way, here, (peer, flip_p, flip_e), source, target in messages:

                @pl.when(here)
                def _():
                    copy(k, frame, way, source, target, flip_p, flip_e, peer).wait_send()

    def clear(slot):
        def zero(i, carry):
            k = i // frames
            stack[(k * 9 + slot) * frames + i - k * frames] = jnp.zeros((basis, LANES), stack.dtype)
            return carry

        lax.fori_loop(0, chunks * frames, zero, 0)

    for name in ("over", "over_near", "over_far", "far", "mate_far"):

        @pl.when(jnp.logical_not(where[name][2]))
        def _():
            clear(slot_of(name))

    pl.semaphore_wait(barrier, count)
    for k in range(chunks):
        for d in range(depth):
            own_loads[k][d].wait()
            start(k, d, [m for m in own(PAST) if k * depth + d < AHEAD])
    for k in range(chunks):
        for d in range(depth):
            keep(k, d, "own")
    for load in loads:
        load.wait()
    whole = inv[...]
    high = whole.astype(jnp.bfloat16)
    low = (whole - high.astype(jnp.float32)).astype(jnp.bfloat16)
    split[...] = jnp.concatenate([high, high, low], axis=1)

    for i in range(nblk):
        place[i] = near_ref[i] * frames + depth - jnp.maximum(lag_ref[i], 1)

    def out_copies(k, step):
        lanes = pl.ds(pl.multiple_of(k * LANES, LANES), LANES)
        part = basis // HALVES
        return [
            pltpu.make_async_copy(
                recv.at[k, 4, depth + step, pl.ds(h * part, part)],
                outs[step * HALVES + h].at[:, lanes],
                out_sem.at[(step * chunks + k) * HALVES + h],
            )
            for h in range(HALVES)
        ]

    def each_step(s, act):
        for step in range(steps):

            @pl.when(s == step)
            def _():
                act(step)

    def write(k, step):
        for move in out_copies(k, step):
            move.start()

    def written(k, step):
        for move in out_copies(k, step):
            move.wait()

    def compute(k, s):
        first = k * 9 * frames + s
        field = jnp.zeros((basis, LANES), jnp.float32)
        for j in range(0, nblk, GROUP):
            sources = []
            for i in range(j, j + GROUP):
                sources.append(stack[first + place[i]])
            field = field + jnp.dot(
                jnp.concatenate([mats[i] for i in range(j, j + GROUP)], axis=1),
                jnp.concatenate(sources, axis=0),
                preferred_element_type=jnp.float32,
            )
        rhs = inc[k, s] - field
        high = rhs.astype(jnp.bfloat16)
        low = (rhs - high.astype(jnp.float32)).astype(jnp.bfloat16)
        current = jnp.dot(
            split[...],
            jnp.concatenate([high, low, high], axis=0),
            preferred_element_type=jnp.float32,
        ).astype(jnp.bfloat16)
        recv[k, 4, depth + s] = current

        @pl.when(s + 1 < steps)
        def _():
            stack[(k * 9 + 4) * frames + depth + s] = current

        @pl.when(s + 1 < steps)
        def _():
            start(k, depth + s, own(NEXT))

        @pl.when(s == steps - 1)
        def _():
            write(k, steps - 1)

    pieces = chunks * depth
    last = LAG + HOLD + pieces - 1

    def piece(i):
        k = i // depth
        return k, i - k * depth

    def body(t, carry):
        @pl.when(t < pieces)
        def _():
            k, d = piece(t)
            after_mate(k, d, PAST)

        @pl.when(t < pieces - AHEAD)
        def _():
            k, d = piece(t + AHEAD)
            start(k, d, [m for m in own(PAST) if True])

        @pl.when(both(t >= LAG, t < LAG + pieces))
        def _():
            k, d = piece(t - LAG)
            after_over(k, d, PAST)

        whole = t - LAG - HOLD + 1
        first = t <= last
        q = jnp.where(first, whole // depth - 1, t - last + chunks - 1)
        s = q // chunks
        k = q - s * chunks

        @pl.when(jnp.logical_not(first))
        def _():
            after_over(k, depth + s - 1, NEXT)
            after_mate(k, depth + s - 1, NEXT)
            @pl.when(q < chunks + pieces)
            def _():
                past_k, past_d = piece(q - chunks)
                drain(past_k, past_d, PAST)

            @pl.when(s >= 2)
            def _():
                drain(k, depth + s - 2, NEXT)

            each_step(s - 1, lambda step: write(k, step))
            each_step(s - 2, lambda step: written(k, step))
            rest(k, depth + s - 1, NEXT)

        ready = both(whole >= depth, lax.rem(whole, depth) == 0)

        @pl.when(both(first, ready))
        def _():
            for d in range(depth):
                rest(k, d, PAST)

        @pl.when(jnp.logical_or(jnp.logical_not(first), ready))
        def _():
            compute(k, s)

        return carry

    lax.fori_loop(0, last + 1 + items - chunks, body, 0)

    def settle(i, carry):
        k, d = piece(i)
        drain(k, d, PAST)
        return carry

    lax.fori_loop(items - chunks, pieces, settle, 0)

    def finish(k, carry):
        drain(k, depth + steps - 2, NEXT)
        written(k, steps - 2)
        written(k, steps - 1)
        return carry

    lax.fori_loop(0, chunks, finish, 0)


def local(rows, cols, history, incident, blocks, self_inverse, neighbour, delay):
    depth, basis, ports = history.shape[2:]
    steps = incident.shape[2]
    nblk = blocks.shape[2]
    chunks = ports // LANES
    items = chunks * steps
    hbm = pl.BlockSpec(memory_space=pl.ANY)
    half = jnp.bfloat16
    currents = pl.pallas_call(
        functools.partial(kernel, rows, cols),
        out_shape=[jax.ShapeDtypeStruct((basis // HALVES, ports), half)] * (steps * HALVES),
        in_specs=[hbm] * 6,
        out_specs=[hbm] * (steps * HALVES),
        scratch_shapes=[
            pltpu.SMEM((nblk,), jnp.int32),
            pltpu.SMEM((nblk,), jnp.int32),
            pltpu.SMEM((nblk,), jnp.int32),
            pltpu.VMEM((chunks, steps, basis, LANES), jnp.float32),
            pltpu.VMEM((nblk, basis, basis), half),
            pltpu.VMEM((basis, basis), jnp.float32),
            pltpu.VMEM((basis, 3 * basis), half),
            pltpu.VMEM((chunks, 9, depth + steps, basis, LANES), half),
            pltpu.VMEM((chunks * 9 * (depth + steps - 1), basis, LANES), half),
            pltpu.SemaphoreType.DMA((chunks * depth + chunks + 4,)),
            pltpu.SemaphoreType.DMA((items * HALVES,)),
            pltpu.SemaphoreType.DMA((chunks * (depth + steps - 1) * 8,)),
            pltpu.SemaphoreType.DMA((chunks * (depth + steps - 1) * 9,)),
        ],
        compiler_params=pltpu.CompilerParams(
            collective_id=0, has_side_effects=True, vmem_limit_bytes=107 * 512 * 1024
        ),
    )(
        neighbour[0, 0],
        delay[0, 0],
        history[0, 0],
        incident[0, 0],
        blocks[0, 0],
        self_inverse[0, 0],
    )
    part = basis // HALVES

    def lay(*refs):
        whole, sem = refs[-2:]
        moves = []
        for i, ref in enumerate(refs[:-2]):
            place = whole.at[i // HALVES, pl.ds(i % HALVES * part, part)]
            moves.append(pltpu.make_async_copy(ref, place, sem.at[i]))
        for move in moves:
            move.start()
        for move in moves:
            move.wait()

    whole = pl.pallas_call(
        lay,
        out_shape=jax.ShapeDtypeStruct((steps, basis, ports), half),
        in_specs=[hbm] * len(currents),
        out_specs=hbm,
        scratch_shapes=[pltpu.SemaphoreType.DMA((len(currents),))],
        compiler_params=pltpu.CompilerParams(vmem_limit_bytes=1024 * 1024),
    )(*currents)
    return whole[None, None]


def solution(mesh):
    in_specs = (
        P("px", "py", None, None, None),
        P("px", "py", None, None, None),
        P("px", "py", None, None, None),
        P("px", "py", None, None),
        P("px", "py", None),
        P("px", "py", None),
    )
    out_specs = P("px", "py", None, None, None)
    body = functools.partial(local, mesh.shape["px"], mesh.shape["py"])
    return jax.shard_map(body, mesh=mesh, in_specs=in_specs, out_specs=out_specs, check_vma=False)
```

```python
import functools

import jax
import jax.numpy as jnp
from jax import lax
from jax.experimental import pallas as pl
from jax.experimental.pallas import tpu as pltpu
from jax.sharding import PartitionSpec as P

MESH = pl.DeviceIdType.MESH
LANES = 128
GROUP = 16
PAST = "RXX"
NEXT = "DDD"


LAG = 4
HOLD = 3
AHEAD = 5
HALVES = 2


def kernel(
    rows,
    cols,
    near_hbm,
    lag_hbm,
    history,
    incident,
    blocks,
    inverse,
    *others,
):
    steps, basis, ports = incident.shape
    outs = others[: HALVES * steps]
    (near_ref, lag_ref, place, inc, mats, inv, split, recv, stack, load_sem, out_sem, send_sem, recv_sem) = others[
        HALVES * steps :
    ]
    depth = history.shape[0]
    nblk = blocks.shape[0]
    chunks = ports // LANES
    items = chunks * steps
    frames = depth + steps - 1
    r = lax.axis_index("px")
    c = lax.axis_index("py")
    p = 1 - 2 * lax.rem(r, 2)
    e = 1 - 2 * lax.rem(c, 2)
    yes = r >= 0
    both = jnp.logical_and

    def inside(index, size):
        return both(index >= 0, index < size)

    has_z = inside(r - p, rows)
    has_on = inside(r + 2 * p, rows)
    has_back = inside(r - 2 * p, rows)
    has_f = inside(c - e, cols)
    mate, over = (r + p, c), (r - p, c)
    near, far = (r, c + e), (r, c - e)
    on, back = (r + 2 * p, c), (r - 2 * p, c)
    mate_far, over_far = (r + p, c - e), (r - p, c - e)
    where = {
        "own": (0, 0, yes),
        "mate": (1, 0, yes),
        "over": (-1, 0, has_z),
        "near": (0, 1, yes),
        "far": (0, -1, has_f),
        "mate_near": (1, 1, yes),
        "over_near": (-1, 1, has_z),
        "mate_far": (1, -1, has_f),
        "over_far": (-1, -1, both(has_z, has_f)),
    }

    def slot_of(name, flip_p=1, flip_e=1):
        a, b, _ = where[name]
        return 4 + 3 * a * flip_p * p + b * flip_e * e

    barrier = pltpu.get_barrier_semaphore()
    greet = (
        (has_z, over),
        (both(has_z, has_f), over_far),
        (yes, mate),
        (has_f, mate_far),
        (has_on, on),
        (has_back, back),
        (has_f, far),
        (yes, near),
    )
    count = 0
    for here, peer in greet:
        count = count + here.astype(jnp.int32)

        @pl.when(here)
        def _():
            pl.semaphore_signal(barrier, inc=1, device_id=peer, device_id_type=MESH)

    own_loads = [
        [
            pltpu.make_async_copy(
                history.at[depth - 1 - d, :, pl.ds(k * LANES, LANES)],
                recv.at[k, 4, d],
                load_sem.at[k * depth + d],
            )
            for d in range(depth)
        ]
        for k in range(chunks)
    ]
    loads = [
        pltpu.make_async_copy(near_hbm, near_ref, load_sem.at[chunks * depth]),
        pltpu.make_async_copy(lag_hbm, lag_ref, load_sem.at[chunks * depth + 1]),
        pltpu.make_async_copy(blocks, mats, load_sem.at[chunks * depth + 2]),
        pltpu.make_async_copy(inverse, inv, load_sem.at[chunks * depth + 3]),
    ]
    for k in range(chunks):
        loads.append(
            pltpu.make_async_copy(
                incident.at[:, :, pl.ds(k * LANES, LANES)], inc.at[k], load_sem.at[chunks * depth + 4 + k]
            )
        )
    for load in sum(own_loads, []) + loads:
        load.start()

    def copy(k, frame, way, source, target, flip_p, flip_e, peer):
        q = frame * chunks + k
        slot = slot_of(target, flip_p, flip_e)
        return pltpu.make_async_remote_copy(
            src_ref=recv.at[k, slot_of(source), frame],
            dst_ref=recv.at[k, slot, frame],
            send_sem=send_sem.at[q * 8 + way],
            recv_sem=recv_sem.at[q * 9 + slot],
            device_id=peer,
            device_id_type=MESH,
        )

    to_mate, to_over, to_on = (mate, -1, 1), (over, -1, 1), (on, 1, 1)
    to_near, to_far = (near, 1, -1), (far, 1, -1)
    to_mate_far, to_over_far = (mate_far, -1, -1), (over_far, -1, -1)

    def start(k, frame, messages):
        for way, here, (peer, flip_p, flip_e), source, target in messages:

            @pl.when(here)
            def _():
                copy(k, frame, way, source, target, flip_p, flip_e, peer).start()

    def landed(k, frame, name):
        @pl.when(where[name][2])
        def _():
            copy(k, frame, 0, name, name, 1, 1, near).wait_recv()

    sides = [(4, yes, to_near, "own", "near"), (5, has_f, to_far, "own", "far")]

    def side_copy(k, way, source, target, flip_p, flip_e, peer):
        slot = slot_of(target, flip_p, flip_e)
        return pltpu.make_async_remote_copy(
            src_ref=recv.at[k, slot_of(source), pl.ds(0, depth)],
            dst_ref=recv.at[k, slot, pl.ds(0, depth)],
            send_sem=send_sem.at[k * 8 + way],
            recv_sem=recv_sem.at[k * 9 + slot],
            device_id=peer,
            device_id_type=MESH,
        )

    def each_side(k, act):
        for way, here, (peer, flip_p, flip_e), source, target in sides:

            @pl.when(here)
            def _():
                act(side_copy(k, way, source, target, flip_p, flip_e, peer))

    def sides_landed(k):
        for name in ("near", "far"):

            @pl.when(where[name][2])
            def _():
                side_copy(k, 0, name, name, 1, 1, near).wait_recv()

            for d in range(depth):
                keep(k, d, name)

    def own(mode):
        messages = []
        if mode[0] == "D":
            messages += [(0, has_z, to_over, "own", "over")]
        if mode[2] == "D":
            messages += [(1, both(has_z, has_f), to_over_far, "own", "over_far")]
        messages += [(2, yes, to_mate, "own", "mate")]
        if mode[1] == "D":
            messages += [(3, has_f, to_mate_far, "own", "mate_far")]
        return messages + (sides if mode == NEXT else [])

    def from_mate(mode):
        messages = []
        if mode[0] == "R":
            messages += [(0, has_on, to_on, "mate", "over")]
        if mode[1] == "X":
            messages += [(3, has_f, to_far, "mate", "mate_far")]
        return messages + [(6, yes, to_near, "mate", "mate_near")]

    def from_mate_far(mode):
        if mode[2] == "R":
            return [(1, both(has_on, has_f), to_on, "mate_far", "over_far")]
        return []

    def from_over(mode):
        messages = []
        if mode[2] == "X":
            messages += [(1, both(has_z, has_f), to_far, "over", "over_far")]
        return messages + [(7, has_z, to_near, "over", "over_near")]

    def after_mate(k, frame, mode):
        landed(k, frame, "mate")
        start(k, frame, from_mate(mode))
        if mode[2] == "R":
            landed(k, frame, "mate_far")
            start(k, frame, from_mate_far(mode))
        keep(k, frame, "mate")

    def after_over(k, frame, mode):
        landed(k, frame, "over")
        start(k, frame, from_over(mode))
        keep(k, frame, "over")

    def keep(k, frame, name):
        @pl.when(where[name][2])
        def _():
            slot = slot_of(name)
            stack[(k * 9 + slot) * frames + frame] = recv[k, slot, frame]

    def rest(k, frame, mode):
        names = ["near", "far", "mate_far", "over_far", "over_near", "mate_near"]
        if mode == PAST:
            names = names[2:]
        if mode[2] == "R":
            names.remove("mate_far")
        for name in names:
            landed(k, frame, name)
            keep(k, frame, name)

    def drain(k, frame, mode):
        for messages in (own(mode), from_mate(mode), from_mate_far(mode), from_over(mode)):
            for way, here, (peer, flip_p, flip_e), source, target in messages:

                @pl.when(here)
                def _():
                    copy(k, frame, way, source, target, flip_p, flip_e, peer).wait_send()

    def clear(slot):
        def zero(i, carry):
            k = i // frames
            stack[(k * 9 + slot) * frames + i - k * frames] = jnp.zeros((basis, LANES), stack.dtype)
            return carry

        lax.fori_loop(0, chunks * frames, zero, 0)

    for name in ("over", "over_near", "over_far", "far", "mate_far"):

        @pl.when(jnp.logical_not(where[name][2]))
        def _():
            clear(slot_of(name))

    pl.semaphore_wait(barrier, count)
    for k in range(chunks):
        for d in range(depth):
            own_loads[k][d].wait()
    for i in range(min(AHEAD, chunks * depth)):
        k, d = i // depth, i % depth
        start(k, d, own(PAST))
        if d == 0:
            each_side(k, lambda move: move.start())
    for k in range(chunks):
        for d in range(depth):
            keep(k, d, "own")
    for load in loads:
        load.wait()
    whole = inv[...]
    high = whole.astype(jnp.bfloat16)
    low = (whole - high.astype(jnp.float32)).astype(jnp.bfloat16)
    split[...] = jnp.concatenate([high, high, low], axis=1)

    for i in range(nblk):
        place[i] = near_ref[i] * frames + depth - jnp.maximum(lag_ref[i], 1)

    def out_copies(k, step):
        lanes = pl.ds(pl.multiple_of(k * LANES, LANES), LANES)
        part = basis // HALVES
        return [
            pltpu.make_async_copy(
                recv.at[k, 4, depth + step, pl.ds(h * part, part)],
                outs[step * HALVES + h].at[:, lanes],
                out_sem.at[(step * chunks + k) * HALVES + h],
            )
            for h in range(HALVES)
        ]

    def each_step(s, act):
        for step in range(steps):

            @pl.when(s == step)
            def _():
                act(step)

    def write(k, step):
        for move in out_copies(k, step):
            move.start()

    def written(k, step):
        for move in out_copies(k, step):
            move.wait()

    def compute(k, s):
        first = k * 9 * frames + s
        field = jnp.zeros((basis, LANES), jnp.float32)
        for j in range(0, nblk, GROUP):
            sources = []
            for i in range(j, j + GROUP):
                sources.append(stack[first + place[i]])
            field = field + jnp.dot(
                jnp.concatenate([mats[i] for i in range(j, j + GROUP)], axis=1),
                jnp.concatenate(sources, axis=0),
                preferred_element_type=jnp.float32,
            )
        rhs = inc[k, s] - field
        high = rhs.astype(jnp.bfloat16)
        low = (rhs - high.astype(jnp.float32)).astype(jnp.bfloat16)
        current = jnp.dot(
            split[...],
            jnp.concatenate([high, low, high], axis=0),
            preferred_element_type=jnp.float32,
        ).astype(jnp.bfloat16)
        recv[k, 4, depth + s] = current

        @pl.when(s + 1 < steps)
        def _():
            stack[(k * 9 + 4) * frames + depth + s] = current

        @pl.when(s + 1 < steps)
        def _():
            start(k, depth + s, own(NEXT))

        @pl.when(s == steps - 1)
        def _():
            write(k, steps - 1)

    pieces = chunks * depth
    last = LAG + HOLD + pieces - 1

    def piece(i):
        k = i // depth
        return k, i - k * depth

    def body(t, carry):
        @pl.when(t < pieces)
        def _():
            k, d = piece(t)
            after_mate(k, d, PAST)

        @pl.when(t < pieces - AHEAD)
        def _():
            k, d = piece(t + AHEAD)
            start(k, d, own(PAST))

            @pl.when(d == 0)
            def _():
                each_side(k, lambda move: move.start())

        @pl.when(both(t >= LAG, t < LAG + pieces))
        def _():
            k, d = piece(t - LAG)
            after_over(k, d, PAST)

        whole = t - LAG - HOLD + 1
        first = t <= last
        q = jnp.where(first, whole // depth - 1, t - last + chunks - 1)
        s = q // chunks
        k = q - s * chunks

        @pl.when(jnp.logical_not(first))
        def _():
            after_over(k, depth + s - 1, NEXT)
            after_mate(k, depth + s - 1, NEXT)
            @pl.when(q < chunks + pieces)
            def _():
                past_k, past_d = piece(q - chunks)
                drain(past_k, past_d, PAST)

                @pl.when(past_d == 0)
                def _():
                    each_side(past_k, lambda move: move.wait_send())

            @pl.when(s >= 2)
            def _():
                drain(k, depth + s - 2, NEXT)

            each_step(s - 1, lambda step: write(k, step))
            each_step(s - 2, lambda step: written(k, step))
            rest(k, depth + s - 1, NEXT)

        ready = both(whole >= depth, lax.rem(whole, depth) == 0)

        @pl.when(both(first, ready))
        def _():
            sides_landed(k)
            for d in range(depth):
                rest(k, d, PAST)

        @pl.when(jnp.logical_or(jnp.logical_not(first), ready))
        def _():
            compute(k, s)

        return carry

    lax.fori_loop(0, last + 1 + items - chunks, body, 0)

    def settle(i, carry):
        k, d = piece(i)
        drain(k, d, PAST)

        @pl.when(d == 0)
        def _():
            each_side(k, lambda move: move.wait_send())

        return carry

    lax.fori_loop(items - chunks, pieces, settle, 0)

    def finish(k, carry):
        drain(k, depth + steps - 2, NEXT)
        written(k, steps - 2)
        written(k, steps - 1)
        return carry

    lax.fori_loop(0, chunks, finish, 0)


def local(rows, cols, history, incident, blocks, self_inverse, neighbour, delay):
    depth, basis, ports = history.shape[2:]
    steps = incident.shape[2]
    nblk = blocks.shape[2]
    chunks = ports // LANES
    items = chunks * steps
    hbm = pl.BlockSpec(memory_space=pl.ANY)
    half = jnp.bfloat16
    currents = pl.pallas_call(
        functools.partial(kernel, rows, cols),
        out_shape=[jax.ShapeDtypeStruct((basis // HALVES, ports), half)] * (steps * HALVES),
        in_specs=[hbm] * 6,
        out_specs=[hbm] * (steps * HALVES),
        scratch_shapes=[
            pltpu.SMEM((nblk,), jnp.int32),
            pltpu.SMEM((nblk,), jnp.int32),
            pltpu.SMEM((nblk,), jnp.int32),
            pltpu.VMEM((chunks, steps, basis, LANES), jnp.float32),
            pltpu.VMEM((nblk, basis, basis), half),
            pltpu.VMEM((basis, basis), jnp.float32),
            pltpu.VMEM((basis, 3 * basis), half),
            pltpu.VMEM((chunks, 9, depth + steps, basis, LANES), half),
            pltpu.VMEM((chunks * 9 * (depth + steps - 1), basis, LANES), half),
            pltpu.SemaphoreType.DMA((chunks * depth + chunks + 4,)),
            pltpu.SemaphoreType.DMA((items * HALVES,)),
            pltpu.SemaphoreType.DMA((chunks * (depth + steps - 1) * 8,)),
            pltpu.SemaphoreType.DMA((chunks * (depth + steps - 1) * 9,)),
        ],
        compiler_params=pltpu.CompilerParams(
            collective_id=0, has_side_effects=True, vmem_limit_bytes=107 * 512 * 1024
        ),
    )(
        neighbour[0, 0],
        delay[0, 0],
        history[0, 0],
        incident[0, 0],
        blocks[0, 0],
        self_inverse[0, 0],
    )
    part = basis // HALVES

    def lay(*refs):
        whole, sem = refs[-2:]
        moves = []
        for i, ref in enumerate(refs[:-2]):
            place = whole.at[i // HALVES, pl.ds(i % HALVES * part, part)]
            moves.append(pltpu.make_async_copy(ref, place, sem.at[i]))
        for move in moves:
            move.start()
        for move in moves:
            move.wait()

    whole = pl.pallas_call(
        lay,
        out_shape=jax.ShapeDtypeStruct((steps, basis, ports), half),
        in_specs=[hbm] * len(currents),
        out_specs=hbm,
        scratch_shapes=[pltpu.SemaphoreType.DMA((len(currents),))],
        compiler_params=pltpu.CompilerParams(vmem_limit_bytes=1024 * 1024),
    )(*currents)
    return whole[None, None]


def solution(mesh):
    in_specs = (
        P("px", "py", None, None, None),
        P("px", "py", None, None, None),
        P("px", "py", None, None, None),
        P("px", "py", None, None),
        P("px", "py", None),
        P("px", "py", None),
    )
    out_specs = P("px", "py", None, None, None)
    body = functools.partial(local, mesh.shape["px"], mesh.shape["py"])
    return jax.shard_map(body, mesh=mesh, in_specs=in_specs, out_specs=out_specs, check_vma=False)
```

```python
import functools

import jax
import jax.numpy as jnp
from jax import lax
from jax.experimental import pallas as pl
from jax.experimental.pallas import tpu as pltpu
from jax.sharding import PartitionSpec as P

MESH = pl.DeviceIdType.MESH
LANES = 128
GROUP = 16
PAST = "RXX"
NEXT = "DDD"


LAG = 4
HOLD = 3
AHEAD = 5
HALVES = 2


def kernel(
    rows,
    cols,
    near_hbm,
    lag_hbm,
    history,
    incident,
    blocks,
    inverse,
    *others,
):
    steps, basis, ports = incident.shape
    outs = others[: HALVES * steps]
    (near_ref, lag_ref, place, inc, mats, inv, split, recv, stack, load_sem, out_sem, send_sem, recv_sem) = others[
        HALVES * steps :
    ]
    depth = history.shape[0]
    nblk = blocks.shape[0]
    chunks = ports // LANES
    items = chunks * steps
    frames = depth + steps - 1
    r = lax.axis_index("px")
    c = lax.axis_index("py")
    p = 1 - 2 * lax.rem(r, 2)
    e = 1 - 2 * lax.rem(c, 2)
    yes = r >= 0
    both = jnp.logical_and

    def inside(index, size):
        return both(index >= 0, index < size)

    has_z = inside(r - p, rows)
    has_on = inside(r + 2 * p, rows)
    has_back = inside(r - 2 * p, rows)
    has_f = inside(c - e, cols)
    mate, over = (r + p, c), (r - p, c)
    near, far = (r, c + e), (r, c - e)
    on, back = (r + 2 * p, c), (r - 2 * p, c)
    mate_far, over_far = (r + p, c - e), (r - p, c - e)
    where = {
        "own": (0, 0, yes),
        "mate": (1, 0, yes),
        "over": (-1, 0, has_z),
        "near": (0, 1, yes),
        "far": (0, -1, has_f),
        "mate_near": (1, 1, yes),
        "over_near": (-1, 1, has_z),
        "mate_far": (1, -1, has_f),
        "over_far": (-1, -1, both(has_z, has_f)),
    }

    def slot_of(name, flip_p=1, flip_e=1):
        a, b, _ = where[name]
        return 4 + 3 * a * flip_p * p + b * flip_e * e

    barrier = pltpu.get_barrier_semaphore()
    greet = (
        (has_z, over),
        (both(has_z, has_f), over_far),
        (yes, mate),
        (has_f, mate_far),
        (has_on, on),
        (has_back, back),
        (has_f, far),
        (yes, near),
    )
    count = 0
    for here, peer in greet:
        count = count + here.astype(jnp.int32)

        @pl.when(here)
        def _():
            pl.semaphore_signal(barrier, inc=1, device_id=peer, device_id_type=MESH)

    own_loads = [
        [
            pltpu.make_async_copy(
                history.at[depth - 1 - d, :, pl.ds(k * LANES, LANES)],
                recv.at[k, 4, d],
                load_sem.at[k * depth + d],
            )
            for d in range(depth)
        ]
        for k in range(chunks)
    ]
    loads = [
        pltpu.make_async_copy(near_hbm, near_ref, load_sem.at[chunks * depth]),
        pltpu.make_async_copy(lag_hbm, lag_ref, load_sem.at[chunks * depth + 1]),
        pltpu.make_async_copy(blocks, mats, load_sem.at[chunks * depth + 2]),
        pltpu.make_async_copy(inverse, inv, load_sem.at[chunks * depth + 3]),
    ]
    for k in range(chunks):
        loads.append(
            pltpu.make_async_copy(
                incident.at[:, :, pl.ds(k * LANES, LANES)], inc.at[k], load_sem.at[chunks * depth + 4 + k]
            )
        )
    for load in sum(own_loads, []) + loads:
        load.start()

    def copy(k, frame, way, source, target, flip_p, flip_e, peer):
        q = frame * chunks + k
        slot = slot_of(target, flip_p, flip_e)
        return pltpu.make_async_remote_copy(
            src_ref=recv.at[k, slot_of(source), frame],
            dst_ref=recv.at[k, slot, frame],
            send_sem=send_sem.at[q * 8 + way],
            recv_sem=recv_sem.at[q * 9 + slot],
            device_id=peer,
            device_id_type=MESH,
        )

    to_mate, to_over, to_on = (mate, -1, 1), (over, -1, 1), (on, 1, 1)
    to_near, to_far = (near, 1, -1), (far, 1, -1)
    to_mate_far, to_over_far = (mate_far, -1, -1), (over_far, -1, -1)

    def start(k, frame, messages):
        for way, here, (peer, flip_p, flip_e), source, target in messages:

            @pl.when(here)
            def _():
                copy(k, frame, way, source, target, flip_p, flip_e, peer).start()

    def landed(k, frame, name):
        @pl.when(where[name][2])
        def _():
            copy(k, frame, 0, name, name, 1, 1, near).wait_recv()

    sides = [(4, yes, to_near, "own", "near"), (5, has_f, to_far, "own", "far")]

    def side_copy(k, way, source, target, flip_p, flip_e, peer):
        slot = slot_of(target, flip_p, flip_e)
        return pltpu.make_async_remote_copy(
            src_ref=recv.at[k, slot_of(source), pl.ds(0, depth)],
            dst_ref=recv.at[k, slot, pl.ds(0, depth)],
            send_sem=send_sem.at[k * 8 + way],
            recv_sem=recv_sem.at[k * 9 + slot],
            device_id=peer,
            device_id_type=MESH,
        )

    def each_side(k, act):
        for way, here, (peer, flip_p, flip_e), source, target in sides:

            @pl.when(here)
            def _():
                act(side_copy(k, way, source, target, flip_p, flip_e, peer))

    def sides_landed(k):
        for name in ("near", "far"):

            @pl.when(where[name][2])
            def _():
                side_copy(k, 0, name, name, 1, 1, near).wait_recv()

            for d in range(depth):
                keep(k, d, name)

    def own(mode):
        messages = []
        messages += [(2, yes, to_mate, "own", "mate")]
        if mode[0] == "D":
            messages += [(0, has_z, to_over, "own", "over")]
        if mode[2] == "D":
            messages += [(1, both(has_z, has_f), to_over_far, "own", "over_far")]
        if mode[1] == "D":
            messages += [(3, has_f, to_mate_far, "own", "mate_far")]
        return messages + (sides if mode == NEXT else [])

    def from_mate(mode):
        messages = []
        if mode[0] == "R":
            messages += [(0, has_on, to_on, "mate", "over")]
        if mode[1] == "X":
            messages += [(3, has_f, to_far, "mate", "mate_far")]
        return messages + [(6, yes, to_near, "mate", "mate_near")]

    def from_mate_far(mode):
        if mode[2] == "R":
            return [(1, both(has_on, has_f), to_on, "mate_far", "over_far")]
        return []

    def from_over(mode):
        messages = []
        if mode[2] == "X":
            messages += [(1, both(has_z, has_f), to_far, "over", "over_far")]
        return messages + [(7, has_z, to_near, "over", "over_near")]

    def after_mate(k, frame, mode):
        landed(k, frame, "mate")
        start(k, frame, from_mate(mode))
        if mode[2] == "R":
            landed(k, frame, "mate_far")
            start(k, frame, from_mate_far(mode))
        keep(k, frame, "mate")

    def after_over(k, frame, mode):
        landed(k, frame, "over")
        start(k, frame, from_over(mode))
        keep(k, frame, "over")

    def keep(k, frame, name):
        @pl.when(where[name][2])
        def _():
            slot = slot_of(name)
            stack[(k * 9 + slot) * frames + frame] = recv[k, slot, frame]

    def rest(k, frame, mode):
        names = ["near", "far", "mate_far", "over_far", "over_near", "mate_near"]
        if mode == PAST:
            names = names[2:]
        if mode[2] == "R":
            names.remove("mate_far")
        for name in names:
            landed(k, frame, name)
            keep(k, frame, name)

    def drain(k, frame, mode):
        for messages in (own(mode), from_mate(mode), from_mate_far(mode), from_over(mode)):
            for way, here, (peer, flip_p, flip_e), source, target in messages:

                @pl.when(here)
                def _():
                    copy(k, frame, way, source, target, flip_p, flip_e, peer).wait_send()

    def clear(slot):
        def zero(i, carry):
            k = i // frames
            stack[(k * 9 + slot) * frames + i - k * frames] = jnp.zeros((basis, LANES), stack.dtype)
            return carry

        lax.fori_loop(0, chunks * frames, zero, 0)

    for name in ("over", "over_near", "over_far", "far", "mate_far"):

        @pl.when(jnp.logical_not(where[name][2]))
        def _():
            clear(slot_of(name))

    pl.semaphore_wait(barrier, count)
    for k in range(chunks):
        for d in range(depth):
            own_loads[k][d].wait()
    for i in range(min(AHEAD, chunks * depth)):
        k, d = i // depth, i % depth
        start(k, d, own(PAST))
        if d == 0:
            each_side(k, lambda move: move.start())
    for k in range(chunks):
        for d in range(depth):
            keep(k, d, "own")
    for load in loads:
        load.wait()
    whole = inv[...]
    high = whole.astype(jnp.bfloat16)
    low = (whole - high.astype(jnp.float32)).astype(jnp.bfloat16)
    split[...] = jnp.concatenate([high, high, low], axis=1)

    for i in range(nblk):
        place[i] = near_ref[i] * frames + depth - jnp.maximum(lag_ref[i], 1)

    def out_copies(k, step):
        lanes = pl.ds(pl.multiple_of(k * LANES, LANES), LANES)
        part = basis // HALVES
        return [
            pltpu.make_async_copy(
                recv.at[k, 4, depth + step, pl.ds(h * part, part)],
                outs[step * HALVES + h].at[:, lanes],
                out_sem.at[(step * chunks + k) * HALVES + h],
            )
            for h in range(HALVES)
        ]

    def each_step(s, act):
        for step in range(steps):

            @pl.when(s == step)
            def _():
                act(step)

    def write(k, step):
        for move in out_copies(k, step):
            move.start()

    def written(k, step):
        for move in out_copies(k, step):
            move.wait()

    def compute(k, s):
        first = k * 9 * frames + s
        field = jnp.zeros((basis, LANES), jnp.float32)
        for j in range(0, nblk, GROUP):
            sources = []
            for i in range(j, j + GROUP):
                sources.append(stack[first + place[i]])
            field = field + jnp.dot(
                jnp.concatenate([mats[i] for i in range(j, j + GROUP)], axis=1),
                jnp.concatenate(sources, axis=0),
                preferred_element_type=jnp.float32,
            )
        rhs = inc[k, s] - field
        high = rhs.astype(jnp.bfloat16)
        low = (rhs - high.astype(jnp.float32)).astype(jnp.bfloat16)
        current = jnp.dot(
            split[...],
            jnp.concatenate([high, low, high], axis=0),
            preferred_element_type=jnp.float32,
        ).astype(jnp.bfloat16)
        recv[k, 4, depth + s] = current

        @pl.when(s + 1 < steps)
        def _():
            stack[(k * 9 + 4) * frames + depth + s] = current

        @pl.when(s + 1 < steps)
        def _():
            start(k, depth + s, own(NEXT))

        @pl.when(s == steps - 1)
        def _():
            write(k, steps - 1)

    pieces = chunks * depth
    last = LAG + HOLD + pieces - 1

    def piece(i):
        k = i // depth
        return k, i - k * depth

    def body(t, carry):
        @pl.when(t < pieces)
        def _():
            k, d = piece(t)
            after_mate(k, d, PAST)

        @pl.when(t < pieces - AHEAD)
        def _():
            k, d = piece(t + AHEAD)
            start(k, d, own(PAST))

            @pl.when(d == 0)
            def _():
                each_side(k, lambda move: move.start())

        @pl.when(both(t >= LAG, t < LAG + pieces))
        def _():
            k, d = piece(t - LAG)
            after_over(k, d, PAST)

        whole = t - LAG - HOLD + 1
        first = t <= last
        q = jnp.where(first, whole // depth - 1, t - last + chunks - 1)
        s = q // chunks
        k = q - s * chunks

        @pl.when(jnp.logical_not(first))
        def _():
            after_over(k, depth + s - 1, NEXT)
            after_mate(k, depth + s - 1, NEXT)
            @pl.when(q < chunks + pieces)
            def _():
                past_k, past_d = piece(q - chunks)
                drain(past_k, past_d, PAST)

                @pl.when(past_d == 0)
                def _():
                    each_side(past_k, lambda move: move.wait_send())

            @pl.when(s >= 2)
            def _():
                drain(k, depth + s - 2, NEXT)

            each_step(s - 1, lambda step: write(k, step))
            each_step(s - 2, lambda step: written(k, step))
            rest(k, depth + s - 1, NEXT)

        ready = both(whole >= depth, lax.rem(whole, depth) == 0)

        @pl.when(both(first, ready))
        def _():
            sides_landed(k)
            for d in range(depth):
                rest(k, d, PAST)

        @pl.when(jnp.logical_or(jnp.logical_not(first), ready))
        def _():
            compute(k, s)

        return carry

    lax.fori_loop(0, last + 1 + items - chunks, body, 0)

    def settle(i, carry):
        k, d = piece(i)
        drain(k, d, PAST)

        @pl.when(d == 0)
        def _():
            each_side(k, lambda move: move.wait_send())

        return carry

    lax.fori_loop(items - chunks, pieces, settle, 0)

    def finish(k, carry):
        drain(k, depth + steps - 2, NEXT)
        written(k, steps - 2)
        written(k, steps - 1)
        return carry

    lax.fori_loop(0, chunks, finish, 0)


def local(rows, cols, history, incident, blocks, self_inverse, neighbour, delay):
    depth, basis, ports = history.shape[2:]
    steps = incident.shape[2]
    nblk = blocks.shape[2]
    chunks = ports // LANES
    items = chunks * steps
    hbm = pl.BlockSpec(memory_space=pl.ANY)
    half = jnp.bfloat16
    currents = pl.pallas_call(
        functools.partial(kernel, rows, cols),
        out_shape=[jax.ShapeDtypeStruct((basis // HALVES, ports), half)] * (steps * HALVES),
        in_specs=[hbm] * 6,
        out_specs=[hbm] * (steps * HALVES),
        scratch_shapes=[
            pltpu.SMEM((nblk,), jnp.int32),
            pltpu.SMEM((nblk,), jnp.int32),
            pltpu.SMEM((nblk,), jnp.int32),
            pltpu.VMEM((chunks, steps, basis, LANES), jnp.float32),
            pltpu.VMEM((nblk, basis, basis), half),
            pltpu.VMEM((basis, basis), jnp.float32),
            pltpu.VMEM((basis, 3 * basis), half),
            pltpu.VMEM((chunks, 9, depth + steps, basis, LANES), half),
            pltpu.VMEM((chunks * 9 * (depth + steps - 1), basis, LANES), half),
            pltpu.SemaphoreType.DMA((chunks * depth + chunks + 4,)),
            pltpu.SemaphoreType.DMA((items * HALVES,)),
            pltpu.SemaphoreType.DMA((chunks * (depth + steps - 1) * 8,)),
            pltpu.SemaphoreType.DMA((chunks * (depth + steps - 1) * 9,)),
        ],
        compiler_params=pltpu.CompilerParams(
            collective_id=0, has_side_effects=True, vmem_limit_bytes=107 * 512 * 1024
        ),
    )(
        neighbour[0, 0],
        delay[0, 0],
        history[0, 0],
        incident[0, 0],
        blocks[0, 0],
        self_inverse[0, 0],
    )
    part = basis // HALVES

    def lay(*refs):
        whole, sem = refs[-2:]
        moves = []
        for i, ref in enumerate(refs[:-2]):
            place = whole.at[i // HALVES, pl.ds(i % HALVES * part, part)]
            moves.append(pltpu.make_async_copy(ref, place, sem.at[i]))
        for move in moves:
            move.start()
        for move in moves:
            move.wait()

    whole = pl.pallas_call(
        lay,
        out_shape=jax.ShapeDtypeStruct((steps, basis, ports), half),
        in_specs=[hbm] * len(currents),
        out_specs=hbm,
        scratch_shapes=[pltpu.SemaphoreType.DMA((len(currents),))],
        compiler_params=pltpu.CompilerParams(vmem_limit_bytes=1024 * 1024),
    )(*currents)
    return whole[None, None]


def solution(mesh):
    in_specs = (
        P("px", "py", None, None, None),
        P("px", "py", None, None, None),
        P("px", "py", None, None, None),
        P("px", "py", None, None),
        P("px", "py", None),
        P("px", "py", None),
    )
    out_specs = P("px", "py", None, None, None)
    body = functools.partial(local, mesh.shape["px"], mesh.shape["py"])
    return jax.shard_map(body, mesh=mesh, in_specs=in_specs, out_specs=out_specs, check_vma=False)
```
